32 devices in a mesh: seq: 8 (over z, x), head: 4 (over y, core).
Axes of the slice: x: 2, y: 2, z: 4, core: 2. Of those that a mesh axis runs over, the one named last changes fastest.
Arguments:
- inputs: float32 [4096, 5120], P('seq', 'head'), may hold values from -3 to 3
- log_decay: float32 [80, 4096], P('head', 'seq'), may hold values from -1 to 0, as said below
- b_proj: float32 [4096, 128], P('seq'), may hold values from -0.5 to 0.5
- c_proj: float32 [4096, 128], P('seq'), may hold values from -0.5 to 0.5
- entry_states: float32 [8, 80, 64, 128], P('seq', 'head'), may hold values from -12 to 12
- out_grad: float32 [4096, 5120], P('seq', 'head'), may hold values from -3 to 3
Outputs:
- d_inputs: float32 [4096, 5120], P('seq', 'head')
- d_log_decay: float32 [80, 4096], P('head', 'seq')
- d_b_proj: float32 [4096, 128], P('seq')
- d_c_proj: float32 [4096, 128], P('seq')
- entry_grad: float32 [8, 80, 64, 128], P('seq', 'head')
The draws below stay inside these ranges and needn't reach their ends.
Inputs may be any that keep to these rules, and one draw needn't show every extreme that they name: `log_decay`: negative everywhere.
All inputs are finite; a program needn't handle non-finite values.
Results may differ from the reference program's by a relative error of at most 0.0003.
Values sent between devices are 32-bit elements; how exact they have to be, the bound alone decides.
A program may use at most 192 MiB of HBM per device.

```python
import jax
import jax.numpy as jnp
from jax import lax

HEAD_TOTAL = 80
HEAD_DIM = 64
D_STATE = 128
BLOCK = 256
TOK_DEV = 512
SHARDS = 8
TOKEN_TOTAL = 4096


def draw_log_decay(key, part):
    random_key_list = jax.random.split(key, 11)
    shard_count = TOKEN_TOTAL // TOK_DEV
    fast_count = max(1, HEAD_TOTAL // 5)
    medium_count = max(1, 3 * HEAD_TOTAL // 10)
    head_rank = jax.random.permutation(random_key_list[0], HEAD_TOTAL)
    fast_flag = head_rank < fast_count
    medium_flag = (head_rank >= fast_count) & (head_rank < fast_count + medium_count)
    slow_flag = head_rank >= fast_count + medium_count
    fast_rate = jax.random.uniform(random_key_list[1], (HEAD_TOTAL,), jnp.float32, 1.0 / 50.0, 1.0 / 30.0)
    slow_rate = 0.2 / TOKEN_TOTAL * jax.random.uniform(random_key_list[2], (HEAD_TOTAL,), jnp.float32, 0.5, 1.0)
    medium_rate = jax.random.uniform(random_key_list[7], (HEAD_TOTAL,), jnp.float32, 1.2, 2.0) / TOK_DEV
    baseline_decay_rate = jnp.where(fast_flag, fast_rate, jnp.where(medium_flag, medium_rate, slow_rate))
    noisy_inputs = jax.random.uniform(random_key_list[3], (HEAD_TOTAL, TOKEN_TOTAL), jnp.float32, 0.5, 2.0)
    shard_multiplier = jax.random.uniform(random_key_list[4], (HEAD_TOTAL, shard_count), jnp.float32, 0.5, 1.0)
    shard_multiplier = jnp.repeat(shard_multiplier, TOK_DEV, axis=1)
    spike_positions = jax.random.randint(random_key_list[5], (3,), 0, TOKEN_TOTAL)
    spike_token_mask = jnp.any(jnp.arange(TOKEN_TOTAL)[None, :] == spike_positions[:, None], axis=0)
    spike_loss_value = jax.random.uniform(random_key_list[6], (HEAD_TOTAL,), jnp.float32, -0.5, -0.22)
    spike_events = jnp.where(slow_flag[:, None] & spike_token_mask[None, :], spike_loss_value[:, None], 0.0)
    baseline = -baseline_decay_rate[:, None] * noisy_inputs * shard_multiplier + spike_events
    strong_pick = jax.random.randint(random_key_list[8], (HEAD_TOTAL, shard_count), 0, 4) == 0
    forced_shard = jax.random.randint(random_key_list[9], (HEAD_TOTAL,), 0, shard_count)
    strong_pick = strong_pick | (jnp.arange(shard_count)[None, :] == forced_shard[:, None])
    strong_tokens = jnp.repeat(strong_pick, TOK_DEV, axis=1) & fast_flag[:, None]
    strong_value = -jax.random.uniform(random_key_list[10], (HEAD_TOTAL, TOKEN_TOTAL), jnp.float32, 0.3, 0.5)
    return jnp.where(strong_tokens, strong_value, baseline).astype(jnp.float32)


def levels(rng, dims, cuts, least, high):
    level = 1.0
    for position, parts in cuts:
        steps = jax.random.uniform(jax.random.fold_in(jax.random.fold_in(rng, 6), position), (parts,), jnp.float32, least / len(cuts), high / len(cuts))
        level = level * jnp.repeat(jnp.exp(steps), dims[position] // parts).reshape((-1,) + (1,) * (len(dims) - 1 - position))
    return level


def bell_draw(key, dims, scale, bound, cuts=(), held_as=jnp.bfloat16):
    array = jax.random.normal(key, dims, jnp.float32) * scale
    if len(cuts) > 0:
        array = levels(key, dims, cuts, -0.22, 0.18) * array
    return jnp.clip(array, min=-bound, max=bound).astype(held_as)


def setup_inputs(seed: int = 0) -> dict:
    key_of = jax.random.split(jax.random.key(seed), 7)
    inputs = bell_draw(key_of[0], (TOKEN_TOTAL, HEAD_TOTAL * HEAD_DIM), 0.5, 3.0, ((0, 8), (1, 4)), jnp.float32)
    log_decay = draw_log_decay(jax.random.fold_in(key_of[6], 71), 0)
    b_proj = bell_draw(key_of[2], (TOKEN_TOTAL, D_STATE), 0.09, 0.5, ((0, 8),), jnp.float32)
    c_proj = bell_draw(key_of[3], (TOKEN_TOTAL, D_STATE), 0.09, 0.5, ((0, 8),), jnp.float32)
    entry_states = bell_draw(key_of[4], (SHARDS, HEAD_TOTAL, HEAD_DIM, D_STATE), 2.0, 12.0, ((0, 8), (1, 4)), jnp.float32)
    out_grad = bell_draw(key_of[5], (TOKEN_TOTAL, HEAD_TOTAL * HEAD_DIM), 0.5, 3.0, ((0, 8), (1, 4)), jnp.float32)
    return {"inputs": inputs, "log_decay": log_decay, "b_proj": b_proj, "c_proj": c_proj, "entry_states": entry_states, "out_grad": out_grad}


def advance(inputs, log_decay, b_proj, c_proj, entry):
    head_count = log_decay.shape[0]
    tok_count = inputs.shape[0]
    head_width = inputs.shape[1] // head_count
    block_count = tok_count // BLOCK
    highest = lax.Precision.HIGHEST
    blocked_in = inputs.reshape(block_count, BLOCK, head_count, head_width)
    rates = log_decay.reshape(head_count, block_count, BLOCK).transpose(1, 0, 2)
    b_blocks = b_proj.reshape(block_count, BLOCK, -1)
    c_blocks = c_proj.reshape(block_count, BLOCK, -1)
    cumulative = jnp.cumsum(rates, axis=2)
    causal = jnp.arange(BLOCK)[:, None] >= jnp.arange(BLOCK)[None, :]
    log_gap = cumulative[:, :, :, None] - cumulative[:, :, None, :]
    decay_table = jnp.where(causal, jnp.exp(jnp.where(causal, log_gap, 0.0)), 0.0)
    scores = jnp.einsum('cln,csn->cls', c_blocks, b_blocks, precision=highest)
    mixing = decay_table * scores[:, None]
    inner_out = jnp.einsum('chls,cshp->clhp', mixing, blocked_in, precision=highest)
    tail_decay = jnp.exp(cumulative[:, :, -1:] - cumulative)
    block_states = jnp.einsum('chs,cshp,csn->chpn', tail_decay, blocked_in, b_blocks, precision=highest)
    totals = jnp.exp(cumulative[:, :, -1])
    current = entry
    entering = []
    for block_index in range(block_count):
        entering.append(current)
        current = totals[block_index][:, None, None] * current + block_states[block_index]
    stacked = jnp.stack(entering)
    outer_out = jnp.einsum('cln,chpn,chl->clhp', c_blocks, stacked, jnp.exp(cumulative), precision=highest)
    return ((inner_out + outer_out).reshape(tok_count, head_count * head_width), current)

def reference(inputs, log_decay, b_proj, c_proj, entry_states, out_grad):
    head_count = log_decay.shape[0]
    shard_in = inputs.reshape(SHARDS, TOK_DEV, -1)
    shard_rates = log_decay.reshape(head_count, SHARDS, TOK_DEV).transpose(1, 0, 2)
    shard_b = b_proj.reshape(SHARDS, TOK_DEV, -1)
    shard_c = c_proj.reshape(SHARDS, TOK_DEV, -1)
    shard_grad = out_grad.reshape(SHARDS, TOK_DEV, -1)

    def backward(later, pieces):
        piece_in, piece_rates, piece_b, piece_c, piece_entry, piece_grad = pieces
        unused, pullback = jax.vjp(advance, piece_in, piece_rates, piece_b, piece_c, piece_entry)
        grads = pullback((piece_grad, later))
        return (grads[4], grads)
    start = jnp.zeros(entry_states.shape[1:], jnp.float32)
    unused, collected = lax.scan(backward, start, (shard_in, shard_rates, shard_b, shard_c, entry_states, shard_grad), reverse=True)
    grad_in, grad_rates, grad_b, grad_c, grad_entry = collected
    d_inputs = grad_in.reshape(TOKEN_TOTAL, -1)
    d_log_decay = grad_rates.transpose(1, 0, 2).reshape(head_count, TOKEN_TOTAL)
    return (d_inputs, d_log_decay, grad_b.reshape(TOKEN_TOTAL, -1), grad_c.reshape(TOKEN_TOTAL, -1), grad_entry)
```

```python
import functools

import jax
import jax.numpy as jnp
from jax import lax
from jax.experimental import pallas as pl
from jax.experimental.pallas import tpu as pltpu
from jax.sharding import PartitionSpec as P

BLOCK = 256
F32 = jnp.float32
BF16 = jnp.bfloat16
NN = (((1,), (0,)), ((), ()))
NT = (((1,), (1,)), ((), ()))
TN = (((0,), (0,)), ((), ()))


def split(value):
    high = value.astype(BF16)
    return high, (value - high.astype(F32)).astype(BF16)


def dot(a, b, dims):
    return lax.dot_general(a, b, dims, preferred_element_type=F32)


def dot3(a, b, dims):
    return dot(a[0], b[0], dims) + dot(a[0], b[1], dims) + dot(a[1], b[0], dims)


def exact(a, b, dims):
    return lax.dot_general(a, b, dims, precision=lax.Precision.HIGHEST, preferred_element_type=F32)


def kernel(
    seq, group, width,
    x_ref, la_ref, b_ref, c_ref, s_ref, dy_ref,
    dx_ref, dla_ref, db_ref, dc_ref, eg_ref,
    acol, arow, score, wsum, bacc, cacc, v, st, local, gbuf, obuf, ey, z, gs, part, rsbuf, red, whole,
    send_sem, recv_sem, rs_send, rs_recv, ag_send, ag_recv,
):
    heads, tok = la_ref.shape
    nb = tok // BLOCK
    lanes = 2 * width
    pairs = heads // 2
    half = BLOCK // 2
    k = lax.axis_index("seq")
    me = lax.axis_index("head")

    barrier = pltpu.get_barrier_semaphore()
    for other in (lax.rem(k + 1, seq), lax.rem(k + seq - 1, seq)):
        pl.semaphore_signal(barrier, inc=1, device_id={"seq": other}, device_id_type=pl.DeviceIdType.MESH)
    for step in range(1, group):
        pl.semaphore_signal(
            barrier, inc=1, device_id={"head": lax.rem(me + step, group)}, device_id_type=pl.DeviceIdType.MESH
        )

    rows_i = lax.broadcasted_iota(jnp.int32, (BLOCK, BLOCK), 0)
    cols_i = lax.broadcasted_iota(jnp.int32, (BLOCK, BLOCK), 1)
    lower = jnp.where(rows_i >= cols_i, 1.0, 0.0).astype(F32)
    upper = jnp.where(rows_i <= cols_i, 1.0, 0.0).astype(F32)
    first = lax.broadcasted_iota(jnp.int32, (BLOCK, lanes), 1) < width

    for b in range(nb):
        span = pl.ds(b * BLOCK, BLOCK)
        rates = la_ref[:, b * BLOCK:(b + 1) * BLOCK]
        sums = exact(rates, upper, NN)
        for h in range(heads):
            arow[h, :, b * BLOCK:(b + 1) * BLOCK] = sums[h:h + 1]
        column = exact(lower, rates, NT)
        for h in range(heads):
            acol[h, span, :] = jnp.broadcast_to(column[:, h:h + 1], (BLOCK, lanes))
        score[b] = jnp.where(rows_i <= cols_i, dot3(split(b_ref[span, :]), split(c_ref[span, :]), NT), 0.0)
    wsum[...] = jnp.zeros_like(wsum)
    bacc[...] = jnp.zeros_like(bacc)
    cacc[...] = jnp.zeros_like(cacc)

    def lane_span(i):
        return pl.ds(pl.multiple_of(i * lanes, lanes), lanes)

    def pair_cum(i, b):
        span = pl.ds(b * BLOCK, BLOCK)
        return jnp.where(first, acol[2 * i, span, :], acol[2 * i + 1, span, :])

    def pair_end(cum):
        return cum[BLOCK - 1:BLOCK, :]

    def row_end(i, b):
        at = pl.ds((b + 1) * BLOCK - 8, 8)
        one = jnp.broadcast_to(acol[2 * i, at, :][7:], (width, lanes))
        two = jnp.broadcast_to(acol[2 * i + 1, at, :][7:], (width, lanes))
        return jnp.concatenate([one, two], axis=0)

    @pl.loop(0, pairs)
    def _(i):
        cols = lane_span(i)
        total = None
        for b in reversed(range(nb)):
            span = pl.ds(b * BLOCK, BLOCK)
            weighted = dy_ref[span, cols] * jnp.exp(pair_cum(i, b))
            value = dot3(split(weighted), split(c_ref[span, :]), TN)
            v[b, cols, :] = value
            total = value if total is None else value + jnp.exp(row_end(i, b)) * total
        local[cols, :] = total

    pl.semaphore_wait(barrier, 2 + group - 1)

    def link(i):
        cols = lane_span(i)
        return pltpu.make_async_remote_copy(
            src_ref=obuf.at[cols, :], dst_ref=gbuf.at[cols, :],
            send_sem=send_sem, recv_sem=recv_sem.at[i],
            device_id={"seq": lax.rem(k + seq - 1, seq)}, device_id_type=pl.DeviceIdType.MESH,
        )

    def chain(i):
        cols = lane_span(i)

        @pl.when(k == seq - 1)
        def _():
            gbuf[cols, :] = jnp.zeros((lanes, gbuf.shape[1]), F32)

        @pl.when(k < seq - 1)
        def _():
            link(i).wait_recv()

        @pl.when(k > 0)
        def _():
            gap = row_end(i, 0)
            for b in range(1, nb):
                gap = gap + row_end(i, b)
            obuf[cols, :] = local[cols, :] + jnp.exp(gap) * gbuf[cols, :]
            link(i).start()

    def before(i):
        cols = lane_span(i)
        state = s_ref[cols, :]
        for b in range(nb):
            span = pl.ds(b * BLOCK, BLOCK)
            st[b, cols, :] = state
            cum = pair_cum(i, b)
            grow = jnp.exp(cum)
            x = x_ref[span, cols]
            dy = dy_ref[span, cols]
            held = split(state)
            bs = split(b_ref[span, :])
            cs = split(c_ref[span, :])
            weighted = dy * grow
            outer = dot3(cs, held, NT)
            ey[span, cols] = weighted * outer
            cacc[span, :] += dot3(split(weighted), held, NN)
            tail = jnp.exp(pair_end(cum) - cum)
            state = jnp.exp(row_end(i, b)) * state + dot3(split(x * tail), bs, TN)

            dy_high, dy_low = split(dy)
            dy_both = jnp.concatenate([dy_high, dy_low], axis=1)
            xr = pltpu.roll(x, width, 1)
            dyr = pltpu.roll(dy, width, 1)
            results = []
            for which in range(2):
                h = 2 * i + which
                own = first if which == 0 else jnp.logical_not(first)
                xd = jnp.where(own, x, xr)
                xh = xd.astype(BF16).astype(F32)
                xm = jnp.where(first, xh, xd - xh).astype(BF16)
                left = jnp.concatenate([xm, xm], axis=1)
                right = jnp.concatenate(split(jnp.where(own, dy, dyr)), axis=1)
                done = []
                qsum = None
                for part_i in range(2):
                    lo = part_i * half
                    n = BLOCK - lo
                    scol = acol[h, pl.ds(b * BLOCK + lo, half), :]
                    if n > lanes:
                        scol = jnp.concatenate([scol] * (n // lanes), axis=1)
                    trow = arow[h, :, b * BLOCK + lo:(b + 1) * BLOCK]
                    decay = jnp.exp(jnp.minimum(trow - scol, 0.0))
                    both = dot(left[lo:lo + half], right[lo:], NT)
                    mix = decay * score[b, lo:lo + half, lo:]
                    wsum[b, lo:lo + half, lo:] += decay * both
                    q = jnp.sum(mix * both, axis=0, keepdims=True)
                    if lo:
                        q = jnp.concatenate([jnp.zeros((1, lo), F32), q], axis=1)
                    qsum = q if qsum is None else qsum + q
                    mh, ml = split(mix)
                    wide = dot(mh, dy_both[lo:], NN)
                    done.append(wide[:, :lanes] + wide[:, lanes:] + dot(ml, dy_high[lo:], NN))
                z[h, :, b * BLOCK:(b + 1) * BLOCK] = qsum
                results.append(jnp.concatenate(done, axis=0))
            dx_ref[span, cols] = jnp.where(first, results[0], results[1])
        st[nb, cols, :] = state

    pick = (
        lax.broadcasted_iota(jnp.int32, (8, lanes), 1) // width
        == lax.broadcasted_iota(jnp.int32, (8, lanes), 0)
    ).astype(BF16)
    pick = jnp.concatenate([pick, pick], axis=1)

    def after(i):
        cols = lane_span(i)
        grad = gbuf[cols, :]
        for b in reversed(range(nb)):
            span = pl.ds(b * BLOCK, BLOCK)
            cum = pair_cum(i, b)
            tail = jnp.exp(pair_end(cum) - cum)
            x = x_ref[span, cols]
            held = split(grad)
            dx = dx_ref[span, cols] + tail * dot3(split(b_ref[span, :]), held, NT)
            dx_ref[span, cols] = dx
            bacc[span, :] += dot3(split(x * tail), held, NN)
            change = jnp.concatenate(split(ey[span, cols] - x * dx), axis=1)
            lines = dot(pick, change, NT)
            prod = grad * st[b + 1, cols, :]
            for which in range(2):
                at = 2 * i + which
                z[at, :, b * BLOCK:(b + 1) * BLOCK] += lines[which:which + 1, :]
                gs[b, at] = jnp.sum(prod[which * width:(which + 1) * width], axis=0, keepdims=True)
            grad = jnp.exp(row_end(i, b)) * grad + v[b, cols, :]
        eg_ref[cols, :] = grad

    @pl.loop(0, pairs + seq - 1)
    def _(i):
        j = i - (seq - 1 - k)
        live = jnp.logical_and(j >= 0, j < pairs)

        @pl.when(live)
        def _():
            chain(j)

        @pl.when(i < pairs)
        def _():
            before(i)

        @pl.when(live)
        def _():
            after(j)

    states = b_ref.shape[1]
    for b in range(nb):
        span = pl.ds(b * BLOCK, BLOCK)
        table = jnp.where(rows_i <= cols_i, wsum[b], 0.0)
        part[span, :states] = bacc[span, :] + exact(table, c_ref[span, :], NN)
        part[span, states:] = cacc[span, :] + exact(table, b_ref[span, :], TN)

    share = tok // group

    def piece(owner):
        return pl.ds(pl.multiple_of(owner * share, share), share)

    def scatter(step):
        to = lax.rem(me + step, group)
        return pltpu.make_async_remote_copy(
            src_ref=part.at[piece(to), :], dst_ref=rsbuf.at[step - 1],
            send_sem=rs_send.at[step - 1], recv_sem=rs_recv.at[step - 1],
            device_id={"head": to}, device_id_type=pl.DeviceIdType.MESH,
        )

    def gather(step):
        to = lax.rem(me + step, group)
        return pltpu.make_async_remote_copy(
            src_ref=red, dst_ref=whole.at[piece(me), :],
            send_sem=ag_send.at[step - 1], recv_sem=ag_recv.at[step - 1],
            device_id={"head": to}, device_id_type=pl.DeviceIdType.MESH,
        )

    for step in range(1, group):
        scatter(step).start()
    for b in range(nb):
        s = slice(b * BLOCK, (b + 1) * BLOCK)
        lines = jnp.concatenate([z[h, :, s] for h in range(heads)], axis=0)
        inner = jnp.concatenate([gs[b, h] for h in range(heads)], axis=0)
        dla_ref[:, s] = exact(lines, lower, NN) + jnp.sum(inner, axis=1, keepdims=True)
    mine = part[piece(me), :]
    for step in range(1, group):
        scatter(step).wait_recv()
        mine = mine + rsbuf[step - 1]
    red[...] = mine
    for step in range(1, group):
        gather(step).start()
    whole[piece(me), :] = mine
    for step in range(1, group):
        gather(step).wait_recv()
    db_ref[...] = whole[:, :states]
    dc_ref[...] = whole[:, states:]
    for step in range(1, group):
        scatter(step).wait_send()
        gather(step).wait_send()

    @pl.when(k > 0)
    def _():
        @pl.loop(0, pairs)
        def _(i):
            link(i).wait_send()


def solution(mesh):
    seq, group = mesh.shape["seq"], mesh.shape["head"]

    def per_device(inputs, log_decay, b_proj, c_proj, entry_states, out_grad):
        heads, tok = log_decay.shape
        full = inputs.shape[1]
        width = full // heads
        states = b_proj.shape[1]
        nb = tok // BLOCK
        lanes = 2 * width
        vm = pl.BlockSpec(memory_space=pltpu.VMEM)
        dx, dla, db, dc, eg = pl.pallas_call(
            functools.partial(kernel, seq, group, width),
            out_shape=[
                jax.ShapeDtypeStruct((tok, full), F32),
                jax.ShapeDtypeStruct((heads, tok), F32),
                jax.ShapeDtypeStruct((tok, states), F32),
                jax.ShapeDtypeStruct((tok, states), F32),
                jax.ShapeDtypeStruct((full, states), F32),
            ],
            in_specs=[vm] * 6,
            out_specs=[vm] * 5,
            scratch_shapes=[
                pltpu.VMEM((heads, tok, lanes), F32),
                pltpu.VMEM((heads, 1, tok), F32),
                pltpu.VMEM((nb, BLOCK, BLOCK), F32),
                pltpu.VMEM((nb, BLOCK, BLOCK), F32),
                pltpu.VMEM((tok, states), F32),
                pltpu.VMEM((tok, states), F32),
                pltpu.VMEM((nb, full, states), F32),
                pltpu.VMEM((nb + 1, full, states), F32),
                pltpu.VMEM((full, states), F32),
                pltpu.VMEM((full, states), F32),
                pltpu.VMEM((full, states), F32),
                pltpu.VMEM((tok, full), F32),
                pltpu.VMEM((heads, 1, tok), F32),
                pltpu.VMEM((nb, heads, 1, states), F32),
                pltpu.VMEM((tok, 2 * states), F32),
                pltpu.VMEM((group - 1, tok // group, 2 * states), F32),
                pltpu.VMEM((tok // group, 2 * states), F32),
                pltpu.VMEM((tok, 2 * states), F32),
                pltpu.SemaphoreType.DMA,
                pltpu.SemaphoreType.DMA((heads // 2,)),
                pltpu.SemaphoreType.DMA((group - 1,)),
                pltpu.SemaphoreType.DMA((group - 1,)),
                pltpu.SemaphoreType.DMA((group - 1,)),
                pltpu.SemaphoreType.DMA((group - 1,)),
            ],
            compiler_params=pltpu.CompilerParams(
                collective_id=0, has_side_effects=True, vmem_limit_bytes=60 * 1024 * 1024
            ),
        )(inputs, log_decay, b_proj, c_proj, entry_states.reshape(full, states), out_grad)
        return dx, dla, db, dc, eg.reshape(entry_states.shape)

    in_specs = (
        P("seq", "head"),
        P("head", "seq"),
        P("seq", None),
        P("seq", None),
        P("seq", "head", None, None),
        P("seq", "head"),
    )
    out_specs = (
        P("seq", "head"),
        P("head", "seq"),
        P("seq", None),
        P("seq", None),
        P("seq", "head", None, None),
    )
    return jax.shard_map(per_device, mesh=mesh, in_specs=in_specs, out_specs=out_specs, check_vma=False)
```

```python
import functools

import jax
import jax.numpy as jnp
from jax import lax
from jax.experimental import pallas as pl
from jax.experimental.pallas import tpu as pltpu
from jax.sharding import PartitionSpec as P

BLOCK = 256
F32 = jnp.float32
BF16 = jnp.bfloat16
NN = (((1,), (0,)), ((), ()))
NT = (((1,), (1,)), ((), ()))
TN = (((0,), (0,)), ((), ()))


def split(value):
    high = value.astype(BF16)
    return high, (value - high.astype(F32)).astype(BF16)


def dot(a, b, dims):
    return lax.dot_general(a, b, dims, preferred_element_type=F32)


def dot3(a, b, dims):
    return dot(a[0], b[0], dims) + dot(a[0], b[1], dims) + dot(a[1], b[0], dims)


def exact(a, b, dims):
    return lax.dot_general(a, b, dims, precision=lax.Precision.HIGHEST, preferred_element_type=F32)


def kernel(
    seq, group, width,
    x_ref, la_ref, b_ref, c_ref, s_ref, dy_ref,
    dx_ref, dla_ref, db_ref, dc_ref, eg_ref,
    acol, arow, score, wsum, bacc, cacc, v, st, local, gbuf, ey, z, gs,
    mine_tot, mate_tot, xbuf, zbuf, zout, gout, part, rsbuf, red, whole,
    t_sem, x_send, x_recv, z_send, z_recv, g_send, g_recv, rs_send, rs_recv, ag_send, ag_recv,
):
    heads, tok = la_ref.shape
    nb = tok // BLOCK
    lanes = 2 * width
    pairs = heads // 2
    half = BLOCK // 2
    k = lax.axis_index("seq")
    me = lax.axis_index("head")

    barrier = pltpu.get_barrier_semaphore()
    late = lax.rem(k, 2)
    mate = k + 1 - 2 * late
    level = k // 2
    levels = seq // 2
    own = pairs // 2
    for other in (mate, lax.rem(k + 2, seq), lax.rem(k + seq - 2, seq)):
        pl.semaphore_signal(barrier, inc=1, device_id={"seq": other}, device_id_type=pl.DeviceIdType.MESH)
    for step in range(1, group):
        pl.semaphore_signal(
            barrier, inc=1, device_id={"head": lax.rem(me + step, group)}, device_id_type=pl.DeviceIdType.MESH
        )

    rows_i = lax.broadcasted_iota(jnp.int32, (BLOCK, BLOCK), 0)
    cols_i = lax.broadcasted_iota(jnp.int32, (BLOCK, BLOCK), 1)
    lower = jnp.where(rows_i >= cols_i, 1.0, 0.0).astype(F32)
    upper = jnp.where(rows_i <= cols_i, 1.0, 0.0).astype(F32)
    first = lax.broadcasted_iota(jnp.int32, (BLOCK, lanes), 1) < width

    for b in range(nb):
        span = pl.ds(b * BLOCK, BLOCK)
        rates = la_ref[:, b * BLOCK:(b + 1) * BLOCK]
        sums = exact(rates, upper, NN)
        for h in range(heads):
            arow[h, :, b * BLOCK:(b + 1) * BLOCK] = sums[h:h + 1]
        column = exact(lower, rates, NT)
        for h in range(heads):
            acol[h, span, :] = jnp.broadcast_to(column[:, h:h + 1], (BLOCK, lanes))
        score[b] = jnp.where(rows_i <= cols_i, dot3(split(b_ref[span, :]), split(c_ref[span, :]), NT), 0.0)
    wsum[...] = jnp.zeros_like(wsum)
    bacc[...] = jnp.zeros_like(bacc)
    cacc[...] = jnp.zeros_like(cacc)

    def lane_span(i):
        return pl.ds(pl.multiple_of(i * lanes, lanes), lanes)

    def pair_cum(i, b):
        span = pl.ds(b * BLOCK, BLOCK)
        return jnp.where(first, acol[2 * i, span, :], acol[2 * i + 1, span, :])

    def pair_end(cum):
        return cum[BLOCK - 1:BLOCK, :]

    def row_end(i, b):
        at = pl.ds((b + 1) * BLOCK - 8, 8)
        one = jnp.broadcast_to(acol[2 * i, at, :][7:], (width, lanes))
        two = jnp.broadcast_to(acol[2 * i + 1, at, :][7:], (width, lanes))
        return jnp.concatenate([one, two], axis=0)

    for h in range(heads):
        total = acol[h, BLOCK - 1:BLOCK, :]
        for b in range(1, nb):
            total = total + acol[h, (b + 1) * BLOCK - 1:(b + 1) * BLOCK, :]
        mine_tot[h] = total

    def remote(src, dst, send, recv, to):
        return pltpu.make_async_remote_copy(
            src_ref=src, dst_ref=dst, send_sem=send, recv_sem=recv,
            device_id={"seq": to}, device_id_type=pl.DeviceIdType.MESH,
        )

    totals = remote(mine_tot, mate_tot, t_sem.at[0], t_sem.at[1], mate)

    def swap(c):
        src = local.at[lane_span(c + (1 - late) * own), :]
        return remote(src, xbuf.at[lane_span(c), :], x_send, x_recv.at[c], mate)

    def climb(c):
        cols = lane_span(c)
        return remote(zout.at[cols, :], zbuf.at[cols, :], z_send, z_recv.at[c], lax.rem(k + seq - 2, seq))

    def hand(c):
        dst = gbuf.at[lane_span(c + late * own), :]
        return remote(gout.at[lane_span(c), :], dst, g_send, g_recv.at[c], mate)

    pl.semaphore_wait(barrier, 3 + group - 1)
    totals.start()

    @pl.loop(0, pairs)
    def _(turn):
        i = lax.rem(turn + (1 - late) * own, pairs)
        cols = lane_span(i)
        total = None
        for b in reversed(range(nb)):
            span = pl.ds(b * BLOCK, BLOCK)
            weighted = dy_ref[span, cols] * jnp.exp(pair_cum(i, b))
            value = dot3(split(weighted), split(c_ref[span, :]), TN)
            v[b, cols, :] = value
            total = value if total is None else value + jnp.exp(row_end(i, b)) * total
        local[cols, :] = total

        @pl.when(turn < own)
        def _():
            swap(turn).start()

    totals.wait()

    def rows_of(ref, i):
        one = jnp.broadcast_to(ref[2 * i], (width, lanes))
        two = jnp.broadcast_to(ref[2 * i + 1], (width, lanes))
        return jnp.concatenate([one, two], axis=0)

    def chain(c):
        i = c + late * own
        cols = lane_span(c)
        here = lane_span(i)

        @pl.when(level == levels - 1)
        def _():
            zbuf[cols, :] = jnp.zeros((lanes, zbuf.shape[1]), F32)

        swap(c).wait_recv()

        @pl.when(level < levels - 1)
        def _():
            climb(c).wait_recv()

        ours, theirs = local[here, :], xbuf[cols, :]
        gap, other = jnp.exp(rows_of(mine_tot, i)), jnp.exp(rows_of(mate_tot, i))
        is_late = late == 1
        above = zbuf[cols, :]
        middle = jnp.where(is_late, ours, theirs) + jnp.where(is_late, gap, other) * above

        @pl.when(level > 0)
        def _():
            zout[cols, :] = jnp.where(is_late, theirs, ours) + jnp.where(is_late, other, gap) * middle
            climb(c).start()

        gout[cols, :] = jnp.where(is_late, middle, above)
        hand(c).start()
        gbuf[here, :] = jnp.where(is_late, above, middle)

    def before(i):
        cols = lane_span(i)
        state = s_ref[cols, :]
        for b in range(nb):
            span = pl.ds(b * BLOCK, BLOCK)
            st[b, cols, :] = state
            cum = pair_cum(i, b)
            grow = jnp.exp(cum)
            x = x_ref[span, cols]
            dy = dy_ref[span, cols]
            held = split(state)
            bs = split(b_ref[span, :])
            cs = split(c_ref[span, :])
            weighted = dy * grow
            outer = dot3(cs, held, NT)
            ey[span, cols] = weighted * outer
            cacc[span, :] += dot3(split(weighted), held, NN)
            tail = jnp.exp(pair_end(cum) - cum)
            state = jnp.exp(row_end(i, b)) * state + dot3(split(x * tail), bs, TN)

            dy_high, dy_low = split(dy)
            dy_both = jnp.concatenate([dy_high, dy_low], axis=1)
            xr = pltpu.roll(x, width, 1)
            dyr = pltpu.roll(dy, width, 1)
            results = []
            for which in range(2):
                h = 2 * i + which
                own = first if which == 0 else jnp.logical_not(first)
                xd = jnp.where(own, x, xr)
                xh = xd.astype(BF16).astype(F32)
                xm = jnp.where(first, xh, xd - xh).astype(BF16)
                left = jnp.concatenate([xm, xm], axis=1)
                right = jnp.concatenate(split(jnp.where(own, dy, dyr)), axis=1)
                done = []
                qsum = None
                for part_i in range(2):
                    lo = part_i * half
                    n = BLOCK - lo
                    scol = acol[h, pl.ds(b * BLOCK + lo, half), :]
                    if n > lanes:
                        scol = jnp.concatenate([scol] * (n // lanes), axis=1)
                    trow = arow[h, :, b * BLOCK + lo:(b + 1) * BLOCK]
                    decay = jnp.exp(jnp.minimum(trow - scol, 0.0))
                    both = dot(left[lo:lo + half], right[lo:], NT)
                    mix = decay * score[b, lo:lo + half, lo:]
                    wsum[b, lo:lo + half, lo:] += decay * both
                    q = jnp.sum(mix * both, axis=0, keepdims=True)
                    if lo:
                        q = jnp.concatenate([jnp.zeros((1, lo), F32), q], axis=1)
                    qsum = q if qsum is None else qsum + q
                    mh, ml = split(mix)
                    wide = dot(mh, dy_both[lo:], NN)
                    done.append(wide[:, :lanes] + wide[:, lanes:] + dot(ml, dy_high[lo:], NN))
                z[h, :, b * BLOCK:(b + 1) * BLOCK] = qsum
                results.append(jnp.concatenate(done, axis=0))
            dx_ref[span, cols] = jnp.where(first, results[0], results[1])
        st[nb, cols, :] = state

    pick = (
        lax.broadcasted_iota(jnp.int32, (8, lanes), 1) // width
        == lax.broadcasted_iota(jnp.int32, (8, lanes), 0)
    ).astype(BF16)
    pick = jnp.concatenate([pick, pick], axis=1)

    def after(i):
        cols = lane_span(i)
        grad = gbuf[cols, :]
        for b in reversed(range(nb)):
            span = pl.ds(b * BLOCK, BLOCK)
            cum = pair_cum(i, b)
            tail = jnp.exp(pair_end(cum) - cum)
            x = x_ref[span, cols]
            held = split(grad)
            dx = dx_ref[span, cols] + tail * dot3(split(b_ref[span, :]), held, NT)
            dx_ref[span, cols] = dx
            bacc[span, :] += dot3(split(x * tail), held, NN)
            change = jnp.concatenate(split(ey[span, cols] - x * dx), axis=1)
            lines = dot(pick, change, NT)
            prod = grad * st[b + 1, cols, :]
            for which in range(2):
                at = 2 * i + which
                z[at, :, b * BLOCK:(b + 1) * BLOCK] += lines[which:which + 1, :]
                gs[b, at] = jnp.sum(prod[which * width:(which + 1) * width], axis=0, keepdims=True)
            grad = jnp.exp(row_end(i, b)) * grad + v[b, cols, :]
        eg_ref[cols, :] = grad

    states = b_ref.shape[1]
    share = tok // group

    def piece(owner):
        return pl.ds(pl.multiple_of(owner * share, share), share)

    def scatter(which, step):
        to = lax.rem(me + step, group)
        return pltpu.make_async_remote_copy(
            src_ref=part.at[which, piece(to), :], dst_ref=rsbuf.at[which, step - 1],
            send_sem=rs_send.at[which, step - 1], recv_sem=rs_recv.at[which, step - 1],
            device_id={"head": to}, device_id_type=pl.DeviceIdType.MESH,
        )

    def gather(which, step):
        to = lax.rem(me + step, group)
        return pltpu.make_async_remote_copy(
            src_ref=red.at[which], dst_ref=whole.at[which, piece(me), :],
            send_sem=ag_send.at[which, step - 1], recv_sem=ag_recv.at[which, step - 1],
            device_id={"head": to}, device_id_type=pl.DeviceIdType.MESH,
        )

    def reduce(which):
        mine = part[which, piece(me), :]
        for step in range(1, group):
            scatter(which, step).wait_recv()
            mine = mine + rsbuf[which, step - 1]
        red[which] = mine
        for step in range(1, group):
            gather(which, step).start()
        whole[which, piece(me), :] = mine

    lag = 1 + 3 * (levels - 1 - level)

    @pl.loop(0, max(pairs, own + 1 + 3 * (levels - 1)))
    def _(turn):
        c = turn - lag
        live = jnp.logical_and(c >= 0, c < own)

        @pl.when(live)
        def _():
            chain(c)

        @pl.when(turn < pairs)
        def _():
            before(lax.rem(turn + late * own, pairs))

        @pl.when(turn == pairs - 1)
        def _():
            for b in range(nb):
                span = pl.ds(b * BLOCK, BLOCK)
                table = split(jnp.where(rows_i <= cols_i, wsum[b], 0.0))
                part[1, span, :] = cacc[span, :] + dot3(table, split(b_ref[span, :]), TN)
                bacc[span, :] += dot3(table, split(c_ref[span, :]), NN)
            for step in range(1, group):
                scatter(1, step).start()

        @pl.when(live)
        def _():
            after(c + late * own)

    reduce(1)

    @pl.loop(0, own)
    def _(c):
        hand(c).wait_recv()
        after(c + (1 - late) * own)

    part[0] = bacc[...]
    for step in range(1, group):
        scatter(0, step).start()
    for b in range(nb):
        s = slice(b * BLOCK, (b + 1) * BLOCK)
        lines = jnp.concatenate([z[h, :, s] for h in range(heads)], axis=0)
        inner = jnp.concatenate([gs[b, h] for h in range(heads)], axis=0)
        dla_ref[:, s] = exact(lines, lower, NN) + jnp.sum(inner, axis=1, keepdims=True)
    reduce(0)
    for which in (1, 0):
        for step in range(1, group):
            gather(which, step).wait_recv()
        out = dc_ref if which else db_ref
        out[...] = whole[which]
    for which in range(2):
        for step in range(1, group):
            scatter(which, step).wait_send()
            gather(which, step).wait_send()

    @pl.loop(0, own)
    def _(c):
        swap(c).wait_send()
        hand(c).wait_send()

    @pl.when(level > 0)
    def _():
        @pl.loop(0, own)
        def _(c):
            climb(c).wait_send()


def solution(mesh):
    seq, group = mesh.shape["seq"], mesh.shape["head"]

    def per_device(inputs, log_decay, b_proj, c_proj, entry_states, out_grad):
        heads, tok = log_decay.shape
        full = inputs.shape[1]
        width = full // heads
        states = b_proj.shape[1]
        nb = tok // BLOCK
        lanes = 2 * width
        vm = pl.BlockSpec(memory_space=pltpu.VMEM)
        dx, dla, db, dc, eg = pl.pallas_call(
            functools.partial(kernel, seq, group, width),
            out_shape=[
                jax.ShapeDtypeStruct((tok, full), F32),
                jax.ShapeDtypeStruct((heads, tok), F32),
                jax.ShapeDtypeStruct((tok, states), F32),
                jax.ShapeDtypeStruct((tok, states), F32),
                jax.ShapeDtypeStruct((full, states), F32),
            ],
            in_specs=[vm] * 6,
            out_specs=[vm] * 5,
            scratch_shapes=[
                pltpu.VMEM((heads, tok, lanes), F32),
                pltpu.VMEM((heads, 1, tok), F32),
                pltpu.VMEM((nb, BLOCK, BLOCK), F32),
                pltpu.VMEM((nb, BLOCK, BLOCK), F32),
                pltpu.VMEM((tok, states), F32),
                pltpu.VMEM((tok, states), F32),
                pltpu.VMEM((nb, full, states), F32),
                pltpu.VMEM((nb + 1, full, states), F32),
                pltpu.VMEM((full, states), F32),
                pltpu.VMEM((full, states), F32),
                pltpu.VMEM((tok, full), F32),
                pltpu.VMEM((heads, 1, tok), F32),
                pltpu.VMEM((nb, heads, 1, states), F32),
                pltpu.VMEM((heads, 1, lanes), F32),
                pltpu.VMEM((heads, 1, lanes), F32),
                pltpu.VMEM((full // 2, states), F32),
                pltpu.VMEM((full // 2, states), F32),
                pltpu.VMEM((full // 2, states), F32),
                pltpu.VMEM((full // 2, states), F32),
                pltpu.VMEM((2, tok, states), F32),
                pltpu.VMEM((2, group - 1, tok // group, states), F32),
                pltpu.VMEM((2, tok // group, states), F32),
                pltpu.VMEM((2, tok, states), F32),
                pltpu.SemaphoreType.DMA((2,)),
                pltpu.SemaphoreType.DMA,
                pltpu.SemaphoreType.DMA((heads // 4,)),
                pltpu.SemaphoreType.DMA,
                pltpu.SemaphoreType.DMA((heads // 4,)),
                pltpu.SemaphoreType.DMA,
                pltpu.SemaphoreType.DMA((heads // 4,)),
                pltpu.SemaphoreType.DMA((2, group - 1)),
                pltpu.SemaphoreType.DMA((2, group - 1)),
                pltpu.SemaphoreType.DMA((2, group - 1)),
                pltpu.SemaphoreType.DMA((2, group - 1)),
            ],
            compiler_params=pltpu.CompilerParams(
                collective_id=0, has_side_effects=True, vmem_limit_bytes=60 * 1024 * 1024
            ),
        )(inputs, log_decay, b_proj, c_proj, entry_states.reshape(full, states), out_grad)
        return dx, dla, db, dc, eg.reshape(entry_states.shape)

    in_specs = (
        P("seq", "head"),
        P("head", "seq"),
        P("seq", None),
        P("seq", None),
        P("seq", "head", None, None),
        P("seq", "head"),
    )
    out_specs = (
        P("seq", "head"),
        P("head", "seq"),
        P("seq", None),
        P("seq", None),
        P("seq", "head", None, None),
    )
    return jax.shard_map(per_device, mesh=mesh, in_specs=in_specs, out_specs=out_specs, check_vma=False)
```

```python
import functools

import jax
import jax.numpy as jnp
from jax import lax
from jax.experimental import pallas as pl
from jax.experimental.pallas import tpu as pltpu
from jax.sharding import PartitionSpec as P

BLOCK = 256
F32 = jnp.float32
BF16 = jnp.bfloat16
NN = (((1,), (0,)), ((), ()))
NT = (((1,), (1,)), ((), ()))
TN = (((0,), (0,)), ((), ()))


def split(value):
    high = value.astype(BF16)
    return high, (value - high.astype(F32)).astype(BF16)


def dot(a, b, dims):
    return lax.dot_general(a, b, dims, preferred_element_type=F32)


def dot3(a, b, dims):
    return dot(a[0], b[0], dims) + dot(a[0], b[1], dims) + dot(a[1], b[0], dims)


def exact(a, b, dims):
    return lax.dot_general(a, b, dims, precision=lax.Precision.HIGHEST, preferred_element_type=F32)


def kernel(
    seq, group, width,
    x_in, la_ref, b_ref, c_ref, s_in, dy_ref,
    dx_out, dla_ref, db_ref, dc_ref, eg_out,
    dx_ref, eg_ref, out_sem, x_ref, s_ref, in_sem,
    acol, arow, score, wsum, bacc, cacc, v, st, local, gbuf, ey, z, gs,
    mine_tot, mate_tot, xbuf, zbuf, zout, gout, part, rsbuf, red, whole,
    t_sem, x_send, x_recv, z_send, z_recv, g_send, g_recv, rs_send, rs_recv, ag_send, ag_recv,
):
    heads, tok = la_ref.shape
    nb = tok // BLOCK
    lanes = 2 * width
    pairs = heads // 2
    half = BLOCK // 2
    k = lax.axis_index("seq")
    me = lax.axis_index("head")

    loads = (
        pltpu.make_async_copy(x_in, x_ref, in_sem.at[0]),
        pltpu.make_async_copy(s_in, s_ref, in_sem.at[1]),
    )
    for load in loads:
        load.start()

    barrier = pltpu.get_barrier_semaphore()
    late = lax.rem(k, 2)
    mate = k + 1 - 2 * late
    level = k // 2
    levels = seq // 2
    own = pairs // 2
    for other in (mate, lax.rem(k + 2, seq), lax.rem(k + seq - 2, seq)):
        pl.semaphore_signal(barrier, inc=1, device_id={"seq": other}, device_id_type=pl.DeviceIdType.MESH)
    for step in range(1, group):
        pl.semaphore_signal(
            barrier, inc=1, device_id={"head": lax.rem(me + step, group)}, device_id_type=pl.DeviceIdType.MESH
        )

    rows_i = lax.broadcasted_iota(jnp.int32, (BLOCK, BLOCK), 0)
    cols_i = lax.broadcasted_iota(jnp.int32, (BLOCK, BLOCK), 1)
    lower = jnp.where(rows_i >= cols_i, 1.0, 0.0).astype(F32)
    upper = jnp.where(rows_i <= cols_i, 1.0, 0.0).astype(F32)
    first = lax.broadcasted_iota(jnp.int32, (BLOCK, lanes), 1) < width

    for b in range(nb):
        span = pl.ds(b * BLOCK, BLOCK)
        rates = la_ref[:, b * BLOCK:(b + 1) * BLOCK]
        sums = exact(rates, upper, NN)
        for h in range(heads):
            arow[h, :, b * BLOCK:(b + 1) * BLOCK] = sums[h:h + 1]
        column = exact(lower, rates, NT)
        for h in range(heads):
            acol[h, span, :] = jnp.broadcast_to(column[:, h:h + 1], (BLOCK, lanes))

    def lane_span(i):
        return pl.ds(pl.multiple_of(i * lanes, lanes), lanes)

    def pair_cum(i, b):
        span = pl.ds(b * BLOCK, BLOCK)
        return jnp.where(first, acol[2 * i, span, :], acol[2 * i + 1, span, :])

    def pair_end(cum):
        return cum[BLOCK - 1:BLOCK, :]

    def row_end(i, b):
        at = pl.ds((b + 1) * BLOCK - 8, 8)
        one = jnp.broadcast_to(acol[2 * i, at, :][7:], (width, lanes))
        two = jnp.broadcast_to(acol[2 * i + 1, at, :][7:], (width, lanes))
        return jnp.concatenate([one, two], axis=0)

    for h in range(heads):
        total = acol[h, BLOCK - 1:BLOCK, :]
        for b in range(1, nb):
            total = total + acol[h, (b + 1) * BLOCK - 1:(b + 1) * BLOCK, :]
        mine_tot[h] = total

    def remote(src, dst, send, recv, to):
        return pltpu.make_async_remote_copy(
            src_ref=src, dst_ref=dst, send_sem=send, recv_sem=recv,
            device_id={"seq": to}, device_id_type=pl.DeviceIdType.MESH,
        )

    totals = remote(mine_tot, mate_tot, t_sem.at[0], t_sem.at[1], mate)

    def swap(c):
        src = local.at[lane_span(c + (1 - late) * own), :]
        return remote(src, xbuf.at[lane_span(c), :], x_send, x_recv.at[c], mate)

    def climb(c):
        cols = lane_span(c)
        return remote(zout.at[cols, :], zbuf.at[cols, :], z_send, z_recv.at[c], lax.rem(k + seq - 2, seq))

    def hand(c):
        dst = gbuf.at[lane_span(c + late * own), :]
        return remote(gout.at[lane_span(c), :], dst, g_send, g_recv.at[c], mate)

    pl.semaphore_wait(barrier, 3 + group - 1)
    totals.start()

    @pl.loop(0, pairs)
    def _(turn):
        i = lax.rem(turn + (1 - late) * own, pairs)
        cols = lane_span(i)
        total = None
        for b in reversed(range(nb)):
            span = pl.ds(b * BLOCK, BLOCK)
            weighted = dy_ref[span, cols] * jnp.exp(pair_cum(i, b))
            value = dot3(split(weighted), split(c_ref[span, :]), TN)
            v[b, cols, :] = value
            total = value if total is None else value + jnp.exp(row_end(i, b)) * total
        local[cols, :] = total

        @pl.when(turn < own)
        def _():
            swap(turn).start()

    for b in range(nb):
        span = pl.ds(b * BLOCK, BLOCK)
        score[b] = jnp.where(rows_i <= cols_i, dot3(split(b_ref[span, :]), split(c_ref[span, :]), NT), 0.0)
    wsum[...] = jnp.zeros_like(wsum)
    bacc[...] = jnp.zeros_like(bacc)
    cacc[...] = jnp.zeros_like(cacc)
    totals.wait()
    for load in loads:
        load.wait()

    def rows_of(ref, i):
        one = jnp.broadcast_to(ref[2 * i], (width, lanes))
        two = jnp.broadcast_to(ref[2 * i + 1], (width, lanes))
        return jnp.concatenate([one, two], axis=0)

    def chain(c):
        i = c + late * own
        cols = lane_span(c)
        here = lane_span(i)

        @pl.when(level == levels - 1)
        def _():
            zbuf[cols, :] = jnp.zeros((lanes, zbuf.shape[1]), F32)

        swap(c).wait_recv()

        @pl.when(level < levels - 1)
        def _():
            climb(c).wait_recv()

        ours, theirs = local[here, :], xbuf[cols, :]
        gap, other = jnp.exp(rows_of(mine_tot, i)), jnp.exp(rows_of(mate_tot, i))
        is_late = late == 1
        above = zbuf[cols, :]
        middle = jnp.where(is_late, ours, theirs) + jnp.where(is_late, gap, other) * above

        @pl.when(level > 0)
        def _():
            zout[cols, :] = jnp.where(is_late, theirs, ours) + jnp.where(is_late, other, gap) * middle
            climb(c).start()

        gout[cols, :] = jnp.where(is_late, middle, above)
        hand(c).start()
        gbuf[here, :] = jnp.where(is_late, above, middle)

    def before(i):
        cols = lane_span(i)
        state = s_ref[cols, :]
        for b in range(nb):
            span = pl.ds(b * BLOCK, BLOCK)
            st[b, cols, :] = state
            cum = pair_cum(i, b)
            grow = jnp.exp(cum)
            x = x_ref[span, cols]
            dy = dy_ref[span, cols]
            held = split(state)
            bs = split(b_ref[span, :])
            cs = split(c_ref[span, :])
            weighted = dy * grow
            outer = dot3(cs, held, NT)
            ey[span, cols] = weighted * outer
            cacc[span, :] += dot3(split(weighted), held, NN)
            tail = jnp.exp(pair_end(cum) - cum)
            state = jnp.exp(row_end(i, b)) * state + dot3(split(x * tail), bs, TN)

            dy_high, dy_low = split(dy)
            dy_both = jnp.concatenate([dy_high, dy_low], axis=1)
            xr = pltpu.roll(x, width, 1)
            dyr = pltpu.roll(dy, width, 1)
            results = []
            for which in range(2):
                h = 2 * i + which
                own = first if which == 0 else jnp.logical_not(first)
                xd = jnp.where(own, x, xr)
                xh = xd.astype(BF16).astype(F32)
                xm = jnp.where(first, xh, xd - xh).astype(BF16)
                left = jnp.concatenate([xm, xm], axis=1)
                right = jnp.concatenate(split(jnp.where(own, dy, dyr)), axis=1)
                done = []
                qsum = None
                for part_i in range(2):
                    lo = part_i * half
                    n = BLOCK - lo
                    scol = acol[h, pl.ds(b * BLOCK + lo, half), :]
                    if n > lanes:
                        scol = jnp.concatenate([scol] * (n // lanes), axis=1)
                    trow = arow[h, :, b * BLOCK + lo:(b + 1) * BLOCK]
                    decay = jnp.exp(jnp.minimum(trow - scol, 0.0))
                    both = dot(left[lo:lo + half], right[lo:], NT)
                    mix = decay * score[b, lo:lo + half, lo:]
                    wsum[b, lo:lo + half, lo:] += decay * both
                    q = jnp.sum(mix * both, axis=0, keepdims=True)
                    if lo:
                        q = jnp.concatenate([jnp.zeros((1, lo), F32), q], axis=1)
                    qsum = q if qsum is None else qsum + q
                    mh, ml = split(mix)
                    wide = dot(mh, dy_both[lo:], NN)
                    done.append(wide[:, :lanes] + wide[:, lanes:] + dot(ml, dy_high[lo:], NN))
                z[h, :, b * BLOCK:(b + 1) * BLOCK] = qsum
                results.append(jnp.concatenate(done, axis=0))
            dx_ref[span, cols] = jnp.where(first, results[0], results[1])
        st[nb, cols, :] = state

    pick = (
        lax.broadcasted_iota(jnp.int32, (8, lanes), 1) // width
        == lax.broadcasted_iota(jnp.int32, (8, lanes), 0)
    ).astype(BF16)
    pick = jnp.concatenate([pick, pick], axis=1)

    def leave(i):
        cols = lane_span(i)
        return (
            pltpu.make_async_copy(dx_ref.at[:, cols], dx_out.at[:, cols], out_sem),
            pltpu.make_async_copy(eg_ref.at[cols, :], eg_out.at[cols, :], out_sem),
        )

    def after(i):
        cols = lane_span(i)
        grad = gbuf[cols, :]
        for b in reversed(range(nb)):
            span = pl.ds(b * BLOCK, BLOCK)
            cum = pair_cum(i, b)
            tail = jnp.exp(pair_end(cum) - cum)
            x = x_ref[span, cols]
            held = split(grad)
            dx = dx_ref[span, cols] + tail * dot3(split(b_ref[span, :]), held, NT)
            dx_ref[span, cols] = dx
            bacc[span, :] += dot3(split(x * tail), held, NN)
            change = jnp.concatenate(split(ey[span, cols] - x * dx), axis=1)
            lines = dot(pick, change, NT)
            prod = grad * st[b + 1, cols, :]
            for which in range(2):
                at = 2 * i + which
                z[at, :, b * BLOCK:(b + 1) * BLOCK] += lines[which:which + 1, :]
                gs[b, at] = jnp.sum(prod[which * width:(which + 1) * width], axis=0, keepdims=True)
            grad = jnp.exp(row_end(i, b)) * grad + v[b, cols, :]
        eg_ref[cols, :] = grad
        for copy in leave(i):
            copy.start()

    states = b_ref.shape[1]
    share = tok // group

    def piece(owner):
        return pl.ds(pl.multiple_of(owner * share, share), share)

    def scatter(which, step):
        to = lax.rem(me + step, group)
        return pltpu.make_async_remote_copy(
            src_ref=part.at[which, piece(to), :], dst_ref=rsbuf.at[which, step - 1],
            send_sem=rs_send.at[which, step - 1], recv_sem=rs_recv.at[which, step - 1],
            device_id={"head": to}, device_id_type=pl.DeviceIdType.MESH,
        )

    def gather(which, step):
        to = lax.rem(me + step, group)
        return pltpu.make_async_remote_copy(
            src_ref=red.at[which], dst_ref=whole.at[which, piece(me), :],
            send_sem=ag_send.at[which, step - 1], recv_sem=ag_recv.at[which, step - 1],
            device_id={"head": to}, device_id_type=pl.DeviceIdType.MESH,
        )

    def reduce(which):
        mine = part[which, piece(me), :]
        for step in range(1, group):
            scatter(which, step).wait_recv()
            mine = mine + rsbuf[which, step - 1]
        red[which] = mine
        for step in range(1, group):
            gather(which, step).start()
        whole[which, piece(me), :] = mine

    lag = 1 + 3 * (levels - 1 - level)

    @pl.loop(0, max(pairs, own + 1 + 3 * (levels - 1)))
    def _(turn):
        c = turn - lag
        live = jnp.logical_and(c >= 0, c < own)

        @pl.when(live)
        def _():
            chain(c)

        @pl.when(turn < pairs)
        def _():
            before(lax.rem(turn + late * own, pairs))

        @pl.when(turn == pairs - 1)
        def _():
            for b in range(nb):
                span = pl.ds(b * BLOCK, BLOCK)
                table = split(jnp.where(rows_i <= cols_i, wsum[b], 0.0))
                part[1, span, :] = cacc[span, :] + dot3(table, split(b_ref[span, :]), TN)
                bacc[span, :] += dot3(table, split(c_ref[span, :]), NN)
            for step in range(1, group):
                scatter(1, step).start()

        @pl.when(live)
        def _():
            after(c + late * own)

    reduce(1)

    @pl.loop(0, own)
    def _(c):
        hand(c).wait_recv()
        after(c + (1 - late) * own)

    part[0] = bacc[...]
    for step in range(1, group):
        scatter(0, step).start()
    for b in range(nb):
        s = slice(b * BLOCK, (b + 1) * BLOCK)
        lines = jnp.concatenate([z[h, :, s] for h in range(heads)], axis=0)
        inner = jnp.concatenate([gs[b, h] for h in range(heads)], axis=0)
        dla_ref[:, s] = exact(lines, lower, NN) + jnp.sum(inner, axis=1, keepdims=True)
    reduce(0)
    for which in (1, 0):
        for step in range(1, group):
            gather(which, step).wait_recv()
        out = dc_ref if which else db_ref
        out[...] = whole[which]
    for which in range(2):
        for step in range(1, group):
            scatter(which, step).wait_send()
            gather(which, step).wait_send()

    @pl.loop(0, pairs)
    def _(i):
        for copy in leave(i):
            copy.wait()

    @pl.loop(0, own)
    def _(c):
        swap(c).wait_send()
        hand(c).wait_send()

    @pl.when(level > 0)
    def _():
        @pl.loop(0, own)
        def _(c):
            climb(c).wait_send()


def solution(mesh):
    seq, group = mesh.shape["seq"], mesh.shape["head"]

    def per_device(inputs, log_decay, b_proj, c_proj, entry_states, out_grad):
        heads, tok = log_decay.shape
        full = inputs.shape[1]
        width = full // heads
        states = b_proj.shape[1]
        nb = tok // BLOCK
        lanes = 2 * width
        vm = pl.BlockSpec(memory_space=pltpu.VMEM)
        hbm = pl.BlockSpec(memory_space=pltpu.HBM)
        dx, dla, db, dc, eg = pl.pallas_call(
            functools.partial(kernel, seq, group, width),
            out_shape=[
                jax.ShapeDtypeStruct((tok, full), F32),
                jax.ShapeDtypeStruct((heads, tok), F32),
                jax.ShapeDtypeStruct((tok, states), F32),
                jax.ShapeDtypeStruct((tok, states), F32),
                jax.ShapeDtypeStruct((full, states), F32),
            ],
            in_specs=[hbm, vm, vm, vm, hbm, vm],
            out_specs=[hbm, vm, vm, vm, hbm],
            scratch_shapes=[
                pltpu.VMEM((tok, full), F32),
                pltpu.VMEM((full, states), F32),
                pltpu.SemaphoreType.DMA,
                pltpu.VMEM((tok, full), F32),
                pltpu.VMEM((full, states), F32),
                pltpu.SemaphoreType.DMA((2,)),
                pltpu.VMEM((heads, tok, lanes), F32),
                pltpu.VMEM((heads, 1, tok), F32),
                pltpu.VMEM((nb, BLOCK, BLOCK), F32),
                pltpu.VMEM((nb, BLOCK, BLOCK), F32),
                pltpu.VMEM((tok, states), F32),
                pltpu.VMEM((tok, states), F32),
                pltpu.VMEM((nb, full, states), F32),
                pltpu.VMEM((nb + 1, full, states), F32),
                pltpu.VMEM((full, states), F32),
                pltpu.VMEM((full, states), F32),
                pltpu.VMEM((tok, full), F32),
                pltpu.VMEM((heads, 1, tok), F32),
                pltpu.VMEM((nb, heads, 1, states), F32),
                pltpu.VMEM((heads, 1, lanes), F32),
                pltpu.VMEM((heads, 1, lanes), F32),
                pltpu.VMEM((full // 2, states), F32),
                pltpu.VMEM((full // 2, states), F32),
                pltpu.VMEM((full // 2, states), F32),
                pltpu.VMEM((full // 2, states), F32),
                pltpu.VMEM((2, tok, states), F32),
                pltpu.VMEM((2, group - 1, tok // group, states), F32),
                pltpu.VMEM((2, tok // group, states), F32),
                pltpu.VMEM((2, tok, states), F32),
                pltpu.SemaphoreType.DMA((2,)),
                pltpu.SemaphoreType.DMA,
                pltpu.SemaphoreType.DMA((heads // 4,)),
                pltpu.SemaphoreType.DMA,
                pltpu.SemaphoreType.DMA((heads // 4,)),
                pltpu.SemaphoreType.DMA,
                pltpu.SemaphoreType.DMA((heads // 4,)),
                pltpu.SemaphoreType.DMA((2, group - 1)),
                pltpu.SemaphoreType.DMA((2, group - 1)),
                pltpu.SemaphoreType.DMA((2, group - 1)),
                pltpu.SemaphoreType.DMA((2, group - 1)),
            ],
            compiler_params=pltpu.CompilerParams(
                collective_id=0, has_side_effects=True, vmem_limit_bytes=60 * 1024 * 1024
            ),
        )(inputs, log_decay, b_proj, c_proj, entry_states.reshape(full, states), out_grad)
        return dx, dla, db, dc, eg.reshape(entry_states.shape)

    in_specs = (
        P("seq", "head"),
        P("head", "seq"),
        P("seq", None),
        P("seq", None),
        P("seq", "head", None, None),
        P("seq", "head"),
    )
    out_specs = (
        P("seq", "head"),
        P("head", "seq"),
        P("seq", None),
        P("seq", None),
        P("seq", "head", None, None),
    )
    return jax.shard_map(per_device, mesh=mesh, in_specs=in_specs, out_specs=out_specs, check_vma=False)
```
